32 devices in a mesh: dp: 8 (over y, x, core), tensor: 4 (over z).
Axes of the slice: x: 2, y: 2, z: 4, core: 2. Of those that a mesh axis runs over, the one named last changes fastest.
Arguments:
- layer_in: bfloat16 [2048, 1024], P('dp', 'tensor'), may hold values from -6 to 6
- layer_cot: bfloat16 [2048, 1024], P('dp', 'tensor'), may hold values from -6 to 6
- segments: int32 [2048], P('dp'), may hold values from 0 to 15, as said below
- positions: int32 [2048], P('dp'), may hold values from 0 to 255, as said below
- counts: int32 [8], P('dp'), may hold values from 64 to 256, as said below
- attn_gain: float32 [1024], replicated, may hold values from 0.25 to 1.75
- w_q: bfloat16 [1024, 2048], P(None, 'tensor'), may hold values from -1 to 1, as said below
- w_k: bfloat16 [1024, 1024], P(None, 'tensor'), may hold values from -1 to 1, as said below
- value_weight: bfloat16 [1024, 1024], P(None, 'tensor'), may hold values from -0.1875 to 0.1875
- q_gain: float32 [128], replicated, may hold values from 0 to 8, as said below
- k_gain: float32 [128], replicated, may hold values from 0 to 8, as said below
- w_o: bfloat16 [2048, 1024], P('tensor'), may hold values from -0.375 to 0.375
- mlp_gain: float32 [1024], replicated, may hold values from 0.25 to 1.75
- w_gate: bfloat16 [1024, 3072], P(None, 'tensor'), may hold values from -0.1875 to 0.1875
- w_up: bfloat16 [1024, 3072], P(None, 'tensor'), may hold values from -0.1875 to 0.1875
- w_down: bfloat16 [3072, 1024], P('tensor'), may hold values from -0.109375 to 0.109375
Outputs:
- layer_out: bfloat16 [2048, 1024], P('dp', 'tensor')
- grad_in: bfloat16 [2048, 1024], P('dp', 'tensor')
- grad_w_q: float32 [1024, 2048], P('dp', 'tensor')
- grad_w_k: float32 [1024, 1024], P('dp', 'tensor')
- grad_w_v: float32 [1024, 1024], P('dp', 'tensor')
- grad_w_o: float32 [2048, 1024], P('tensor', 'dp')
- grad_w_gate: float32 [1024, 3072], P('dp', 'tensor')
- grad_w_up: float32 [1024, 3072], P('dp', 'tensor')
- grad_w_down: float32 [3072, 1024], P('tensor', 'dp')
- grad_attn_gain: float32 [1024], P('dp')
- grad_mlp_gain: float32 [1024], P('dp')
- grad_q_gain: float32 [128], P('dp')
- grad_k_gain: float32 [128], P('dp')
The draws below stay inside these ranges and needn't reach their ends.
Inputs may be any that keep to these rules, and one draw needn't show every extreme that they name: Within each block of 256 tokens segment numbers start at 0 and never fall, and a segment begins only at a multiple of 16 within its block; a sequence is one segment of one block; some block holds 16 segments. `positions`: A token's position counts from 0 at the first token of its segment; some block is a single segment. `counts`: the valid tokens of a block are its first ones; some block is full and some holds 64. `w_q`: projection weights. `w_k`: projection weights. `q_gain`: positive gains. `k_gain`: positive gains.
All inputs are finite; a program needn't handle non-finite values.
Results may differ from the reference program's by a relative error of at most 0.02.
The reference program's roundings to bfloat16 on the way count: a program that leaves them out, or rounds other values in their place, can miss the bound.
Values may be sent and summed in bfloat16 or wider, within the bound.
No kernel may reach another device: no remote copies, remote signals or barrier semaphores. Data moves between devices by JAX's collectives and lax.ppermute only.
A program may use at most 128 MiB of HBM per device.

```python
import jax
import jax.numpy as jnp
from jax import lax

MODEL_WIDTH = 1024
QUERY_HEADS = 16
KEY_VALUE_HEADS = 8
HEAD_SIZE = 128
FF = 3072
CAP = 256
TOKENS = 2048
N_DP = 8


def query_offset_start(key):
    regular_portion = jax.random.normal(jax.random.fold_in(key, 101), (MODEL_WIDTH, QUERY_HEADS * HEAD_SIZE), jnp.float32)
    return jnp.clip(regular_portion, -6.0, 6.0) * MODEL_WIDTH ** (-0.5)


def draw_w_q(key, part):
    return query_offset_start(key).astype(jnp.bfloat16)


def draw_w_k(key, part):
    regular_portion = jax.random.normal(jax.random.fold_in(key, 202), (MODEL_WIDTH, KEY_VALUE_HEADS * HEAD_SIZE), jnp.float32)
    own_part = jnp.clip(regular_portion, -6.0, 6.0) * MODEL_WIDTH ** (-0.5)
    return own_part.astype(jnp.bfloat16)


def head_gain(key, salt):
    sub_key = jax.random.fold_in(key, salt)
    return jax.random.uniform(sub_key, (HEAD_SIZE,), jnp.float32, 0.6, 1.8)


def draw_q_gain(key, part):
    return head_gain(key, 303)


def draw_k_gain(key, part):
    return head_gain(key, 404)


def block_layout(key):
    grains = 16
    width = CAP // grains
    rolls = jax.random.randint(jax.random.fold_in(key, 505), (N_DP, grains), 0, 4)
    grain_index = jnp.arange(grains, dtype=jnp.int32)
    block_index = jnp.arange(N_DP, dtype=jnp.int32)[:, None]
    grain_starts = (rolls == 0) | (grain_index[None, :] == 0)
    grain_starts = jnp.where(block_index == 0, True, jnp.where(block_index == 1, grain_index[None, :] == 0, grain_starts))
    index = jnp.arange(CAP, dtype=jnp.int32)
    starts = jnp.repeat(grain_starts, width, axis=1) & (index % width == 0)[None, :]
    segment_ids = jnp.cumsum(starts.astype(jnp.int32), axis=1) - 1
    start_at = lax.cummax(jnp.where(starts, index[None, :], 0), axis=1)
    offsets = index[None, :] - start_at
    return (segment_ids.reshape(N_DP * CAP).astype(jnp.int32), offsets.reshape(N_DP * CAP).astype(jnp.int32))


def draw_segments(key, part):
    return block_layout(key)[0]


def draw_positions(key, part):
    return block_layout(key)[1]


def draw_counts(key, part):
    first_key = jax.random.fold_in(key, 606)
    second_key = jax.random.fold_in(key, 707)
    third_key = jax.random.fold_in(key, 808)
    base = jax.random.randint(first_key, (N_DP,), CAP // 4, CAP + 1)
    fullest = jax.random.randint(second_key, (), 0, N_DP)
    lightest = (fullest + 1 + jax.random.randint(third_key, (), 0, N_DP - 1)) % N_DP
    index = jnp.arange(N_DP, dtype=jnp.int32)
    return jnp.where(index == fullest, CAP, jnp.where(index == lightest, CAP // 4, base)).astype(jnp.int32)


def raised(array, own_key, source, target, blocks, factor):
    owner, partner = [(jnp.arange(array.shape[position]) // (array.shape[position] // blocks)).reshape([-1 if axis == position else 1 for axis in range(array.ndim)]) for position in (source, target)]
    chosen = jax.random.permutation(own_key, blocks)[partner]
    strong = (owner == chosen) | (owner == (partner + blocks // 2) % blocks)
    return jnp.where(strong, factor * array, array)


def shard_levels(own_key, shape, pieces, smallest, top_value):
    level, own = 1.0, jax.random.fold_in(own_key, 6)
    for dim, shards_of in pieces:
        steps = jnp.exp(jax.random.uniform(jax.random.fold_in(own, dim), (shards_of,), jnp.float32, smallest / len(pieces), top_value / len(pieces)))
        level = level * jnp.repeat(steps, shape[dim] // shards_of).reshape([-1 if axis == dim else 1 for axis in range(len(shape))])
    return level


def scatter_about(key, shape, deviation, reach, pieces=(), held_as=jnp.bfloat16):
    factor_of = shard_levels(key, shape, pieces, -0.22, 0.18) if pieces else 1.0
    array = jax.random.normal(key, shape, jnp.float32) * deviation * factor_of
    return jnp.minimum(jnp.maximum(array, -reach), reach).astype(held_as)


def noise_with(own_key, extent, spread, reach, shards, heavy, held_as=jnp.bfloat16):
    values = spread * jax.random.normal(own_key, extent, jnp.float32)
    if shards:
        values = values * shard_levels(own_key, extent, shards, -0.22, 0.18)
    return jnp.clip(raised(values, jax.random.fold_in(own_key, 3), *heavy), -reach, reach).astype(held_as)


def setup_inputs(seed: int = 0) -> dict:
    key_list = jax.random.split(jax.random.key(seed), 17)
    return {
        "layer_in": scatter_about(key_list[0], (TOKENS, MODEL_WIDTH), 1.0, 6.0, ((0, 8), (1, 4))),
        "layer_cot": noise_with(key_list[1], (TOKENS, MODEL_WIDTH), 1.0, 6.0, ((0, 8), (1, 4)), (0, 1, 8, 2.0)),
        "segments": draw_segments(jax.random.fold_in(key_list[16], 71), 0),
        "positions": draw_positions(jax.random.fold_in(key_list[16], 71), 0),
        "counts": draw_counts(jax.random.fold_in(key_list[16], 71), 0),
        "attn_gain": jnp.clip(1.0 + 0.15 * jax.random.normal(key_list[5], (MODEL_WIDTH,), jnp.float32), 0.25, 1.75),
        "w_q": draw_w_q(jax.random.fold_in(key_list[16], 71), 0),
        "w_k": draw_w_k(jax.random.fold_in(key_list[16], 71), 0),
        "value_weight": scatter_about(key_list[8], (MODEL_WIDTH, KEY_VALUE_HEADS * HEAD_SIZE), MODEL_WIDTH ** -0.5, 0.1875, ((1, 4),)),
        "q_gain": draw_q_gain(jax.random.fold_in(key_list[16], 71), 0),
        "k_gain": draw_k_gain(jax.random.fold_in(key_list[16], 71), 0),
        "w_o": scatter_about(key_list[11], (QUERY_HEADS * HEAD_SIZE, MODEL_WIDTH), (QUERY_HEADS * HEAD_SIZE // 8) ** -0.5, 0.375, ((0, 4),)),
        "mlp_gain": jnp.clip(1.0 + 0.15 * jax.random.normal(key_list[12], (MODEL_WIDTH,), jnp.float32), 0.25, 1.75),
        "w_gate": scatter_about(key_list[13], (MODEL_WIDTH, FF), MODEL_WIDTH ** -0.5, 0.1875, ((1, 4),)),
        "w_up": scatter_about(key_list[14], (MODEL_WIDTH, FF), MODEL_WIDTH ** -0.5, 0.1875, ((1, 4),)),
        "w_down": scatter_about(key_list[15], (FF, MODEL_WIDTH), FF ** -0.5, 0.109375, ((0, 4),)),
    }


EPSILON = 1e-06
THETA = 1000000.0

def mult(left, right):
    return jnp.dot(left, right, preferred_element_type=jnp.float32)

def inv_rms(values):
    return lax.rsqrt(lax.optimization_barrier(jnp.mean(values * values, axis=-1, keepdims=True)) + EPSILON)

def rotary_tables(positions):
    half = HEAD_SIZE // 2
    freq = THETA ** (-(jnp.arange(half, dtype=jnp.float32) * 2.0 / HEAD_SIZE))
    angle = positions.astype(jnp.float32)[:, None] * freq[None, :]
    return (jnp.cos(angle)[:, None, :], jnp.sin(angle)[:, None, :])

def head_prep(linear, gain, cosine, sine):
    normed = linear * inv_rms(linear) * gain
    half = normed.shape[-1] // 2
    first = normed[..., :half]
    second = normed[..., half:]
    return jnp.concatenate([first * cosine - second * sine, second * cosine + first * sine], axis=-1)

def allowed_mask(segments, count):
    rows = segments.shape[0]
    index = jnp.arange(rows, dtype=jnp.int32)
    same = segments[:, None] == segments[None, :]
    before = index[None, :] < index[:, None]
    live = index[:, None] < count
    return (index[:, None] == index[None, :]) | same & before & live

def scores_of(queries, keys, mask, factor):
    scores = jnp.einsum('ikgd,jkd->kgij', queries.astype(jnp.float32), keys.astype(jnp.float32)) * factor
    return jnp.where(mask[None, None], scores, -1e+30)

def layer_block(layer_in, layer_cot, segments, positions, count, attn_gain, w_q, w_k, value_weight, q_gain, k_gain, w_o, mlp_gain, w_gate, w_up, w_down):
    rows = layer_in.shape[0]
    q_heads = w_q.shape[1] // HEAD_SIZE
    kv_heads = w_k.shape[1] // HEAD_SIZE
    group = q_heads // kv_heads
    factor = HEAD_SIZE ** (-0.5)
    live_rows = (jnp.arange(rows, dtype=jnp.int32) < count).astype(jnp.float32)[:, None]
    mask = allowed_mask(segments, count)
    cosine, sine = rotary_tables(positions)
    in_float = layer_in.astype(jnp.float32)
    scale_one = inv_rms(in_float)
    normed_one = (in_float * scale_one * attn_gain).astype(jnp.bfloat16)
    q_lin = mult(normed_one, w_q).reshape(rows, q_heads, HEAD_SIZE)
    k_lin = mult(normed_one, w_k).reshape(rows, kv_heads, HEAD_SIZE)
    values = mult(normed_one, value_weight).astype(jnp.bfloat16).reshape(rows, kv_heads, HEAD_SIZE)

    def prep_fn(linear, gain):
        return head_prep(linear, gain, cosine, sine)
    queries_f, back_query = jax.vjp(prep_fn, q_lin, q_gain)
    keys_f, back_key = jax.vjp(prep_fn, k_lin, k_gain)
    queries = queries_f.astype(jnp.bfloat16).reshape(rows, kv_heads, group, HEAD_SIZE)
    keys = keys_f.astype(jnp.bfloat16)
    scores = scores_of(queries, keys, mask, factor)
    peak = lax.optimization_barrier(jnp.max(scores, axis=-1, keepdims=True))
    lse = peak + jnp.log(lax.optimization_barrier(jnp.sum(jnp.exp(scores - peak), axis=-1, keepdims=True)))
    probs_f = jnp.exp(scores - lse)
    attn_probs = probs_f.astype(jnp.bfloat16)
    attended4 = jnp.einsum('kgij,jkd->ikgd', attn_probs.astype(jnp.float32), values.astype(jnp.float32)).astype(jnp.bfloat16)
    attended = attended4.reshape(rows, q_heads * HEAD_SIZE)
    residual = in_float + mult(attended, w_o)
    scale_two = inv_rms(residual)
    normed_two = (residual * scale_two * mlp_gain).astype(jnp.bfloat16)
    gate_lin = mult(normed_two, w_gate)
    up_lin = mult(normed_two, w_up)
    sigmoid_gate = jax.nn.sigmoid(gate_lin)
    silu_gate = gate_lin * sigmoid_gate
    hidden = (silu_gate * up_lin).astype(jnp.bfloat16)
    layer_out = ((residual + mult(hidden, w_down)) * live_rows).astype(jnp.bfloat16)
    grad_out = layer_cot * live_rows.astype(layer_cot.dtype)
    d_hidden = mult(grad_out, w_down.T)
    d_gate = (d_hidden * up_lin * sigmoid_gate * (1.0 + gate_lin * (1.0 - sigmoid_gate))).astype(jnp.bfloat16)
    d_up = (d_hidden * silu_gate).astype(jnp.bfloat16)
    d_normed_two = mult(d_gate, w_gate.T) + mult(d_up, w_up.T)
    grad_mlp_gain = lax.optimization_barrier(jnp.sum(d_normed_two * residual * scale_two, axis=0))
    gained_two = d_normed_two * mlp_gain
    d_residual = grad_out.astype(jnp.float32) + scale_two * gained_two - residual * scale_two ** 3 * lax.optimization_barrier(jnp.mean(gained_two * residual, axis=-1, keepdims=True))
    d_res_b = d_residual.astype(jnp.bfloat16)
    grad_w_o = mult(attended.T, d_res_b)
    grad_w_down = mult(hidden.T, grad_out)
    grad_w_gate = mult(normed_two.T, d_gate)
    grad_w_up = mult(normed_two.T, d_up)
    d_attended = mult(d_res_b, w_o.T).astype(jnp.bfloat16).reshape(rows, kv_heads, group, HEAD_SIZE)
    d_att_f = d_attended.astype(jnp.float32)
    delta = jnp.einsum('ikgd,ikgd->kgi', d_att_f, attended4.astype(jnp.float32))[..., None]
    d_probs = jnp.einsum('ikgd,jkd->kgij', d_att_f, values.astype(jnp.float32))
    d_scores = (probs_f * (d_probs - delta)).astype(jnp.bfloat16).astype(jnp.float32)
    d_values = jnp.einsum('kgij,ikgd->jkd', attn_probs.astype(jnp.float32), d_att_f)
    d_queries = jnp.einsum('kgij,jkd->ikgd', d_scores, keys.astype(jnp.float32)) * factor
    d_keys = jnp.einsum('kgij,ikgd->jkd', d_scores, queries.astype(jnp.float32)) * factor
    d_q_lin, grad_q_gain = back_query(d_queries.reshape(rows, q_heads, HEAD_SIZE))
    d_k_lin, grad_k_gain = back_key(d_keys)
    d_q_b = d_q_lin.reshape(rows, q_heads * HEAD_SIZE).astype(jnp.bfloat16)
    d_k_b = d_k_lin.reshape(rows, kv_heads * HEAD_SIZE).astype(jnp.bfloat16)
    d_v_b = d_values.reshape(rows, kv_heads * HEAD_SIZE).astype(jnp.bfloat16)
    grad_w_q = mult(normed_one.T, d_q_b)
    grad_w_k = mult(normed_one.T, d_k_b)
    grad_w_v = mult(normed_one.T, d_v_b)
    d_normed_one = mult(d_q_b, w_q.T) + mult(d_k_b, w_k.T) + mult(d_v_b, value_weight.T)
    grad_attn_gain = lax.optimization_barrier(jnp.sum(d_normed_one * in_float * scale_one, axis=0))
    gained_one = d_normed_one * attn_gain
    grad_in = (d_residual + scale_one * gained_one - in_float * scale_one ** 3 * lax.optimization_barrier(jnp.mean(gained_one * in_float, axis=-1, keepdims=True))).astype(jnp.bfloat16)
    return (layer_out, grad_in, (grad_w_q, grad_w_k, grad_w_v, grad_w_o, grad_w_gate, grad_w_up, grad_w_down, grad_attn_gain, grad_mlp_gain, grad_q_gain, grad_k_gain))

def reference(layer_in, layer_cot, segments, positions, counts, attn_gain, w_q, w_k, value_weight, q_gain, k_gain, w_o, mlp_gain, w_gate, w_up, w_down):
    shaped = (layer_in.reshape(N_DP, CAP, MODEL_WIDTH), layer_cot.reshape(N_DP, CAP, MODEL_WIDTH), segments.reshape(N_DP, CAP), positions.reshape(N_DP, CAP), counts)
    params = (w_q, w_k, value_weight, w_o, w_gate, w_up, w_down, attn_gain, mlp_gain, q_gain, k_gain)
    initial = tuple((jnp.zeros(param.shape, jnp.float32) for param in params))

    def step(carry, block):
        block_out, block_grad, grads = layer_block(block[0], block[1], block[2], block[3], block[4], attn_gain, w_q, w_k, value_weight, q_gain, k_gain, w_o, mlp_gain, w_gate, w_up, w_down)
        return (jax.tree.map(jnp.add, carry, grads), (block_out, block_grad))
    totals, stacked = lax.scan(step, initial, shaped)
    layer_out = stacked[0].reshape(N_DP * CAP, MODEL_WIDTH)
    grad_in = stacked[1].reshape(N_DP * CAP, MODEL_WIDTH)
    return (layer_out, grad_in, totals[0], totals[1], totals[2], totals[3], totals[4], totals[5], totals[6], totals[7], totals[8], totals[9], totals[10])
```

```python
import jax
import jax.numpy as jnp
from jax import lax
from jax.sharding import PartitionSpec as P

HEAD_SIZE = 128


EPSILON = 1e-06
THETA = 1000000.0


def mult(left, right):
    return jnp.dot(left, right, preferred_element_type=jnp.float32)


def inv_rms(values):
    return lax.rsqrt(jnp.mean(values * values, axis=-1, keepdims=True) + EPSILON)


def rotary_tables(positions):
    half = HEAD_SIZE // 2
    freq = THETA ** (-(jnp.arange(half, dtype=jnp.float32) * 2.0 / HEAD_SIZE))
    angle = positions.astype(jnp.float32)[:, None] * freq[None, :]
    return (jnp.cos(angle)[:, None, :], jnp.sin(angle)[:, None, :])


def head_prep(linear, gain, cosine, sine):
    normed = linear * inv_rms(linear) * gain
    half = normed.shape[-1] // 2
    first = normed[..., :half]
    second = normed[..., half:]
    return jnp.concatenate(
        [first * cosine - second * sine, second * cosine + first * sine], axis=-1
    )


def allowed_mask(segments, count):
    rows = segments.shape[0]
    index = jnp.arange(rows, dtype=jnp.int32)
    same = segments[:, None] == segments[None, :]
    before = index[None, :] < index[:, None]
    live = index[:, None] < count
    return (index[:, None] == index[None, :]) | same & before & live


def scores_of(queries, keys, mask, factor):
    scores = (
        jnp.einsum("ikgd,jkd->kgij", queries, keys, preferred_element_type=jnp.float32) * factor
    )
    return jnp.where(mask[None, None], scores, -1e30)


def swap_with(value, axis, size, bit):
    return lax.ppermute(value, axis, [(i, i ^ bit) for i in range(size)])


def relative_blocks(blocks, index):
    count = len(blocks)
    bit = 1
    while bit < count:
        flip = (index & bit) != 0
        blocks = [jnp.where(flip, blocks[r ^ bit], blocks[r]) for r in range(count)]
        bit *= 2
    return blocks


def gather_pieces(piece, size):
    return [piece] + [swap_with(piece, "tensor", size, k) for k in range(1, size)]


def gather_columns(piece, index, size):
    return jnp.concatenate(relative_blocks(gather_pieces(piece, size), index), axis=1)


def scatter_columns(partial, index, size):
    share = partial.shape[1] // size

    def block(k):
        return lax.dynamic_slice_in_dim(partial, (index ^ k) * share, share, 1)

    received = [
        swap_with(block(k).astype(jnp.bfloat16), "tensor", size, k) for k in range(1, size)
    ]
    total = block(0).astype(jnp.float32)
    for part in received:
        total = total + part.astype(jnp.float32)
    return total


def relative_columns(array, index, size):
    width = array.shape[1] // size
    blocks = [array[:, r * width : (r + 1) * width] for r in range(size)]
    return relative_blocks(blocks, index)


def transposed_mult(left, right):
    return lax.dot_general(
        left, right, (((0,), (0,)), ((), ())), preferred_element_type=jnp.float32
    )


def bit_orders(size):
    bits = []
    bit = 2
    while bit < size:
        bits.append(bit)
        bit *= 2
    return bits, bits[::-1]


def halve(rows_by_r, bits, size):
    for bit in bits:
        sent_keys = [r for r in rows_by_r if r & bit]
        kept_keys = [r for r in rows_by_r if not r & bit]
        sent = jnp.concatenate([rows_by_r[r] for r in sent_keys], axis=0).astype(jnp.bfloat16)
        got = swap_with(sent, "dp", size, bit).astype(jnp.float32)
        width = got.shape[0] // len(kept_keys)
        rows_by_r = {
            r: rows_by_r[r] + got[i * width : (i + 1) * width] for i, r in enumerate(kept_keys)
        }
    return rows_by_r[0]


def summed_gradient(left_blocks, right, size, routes):
    odd = [r for r in range(size) if r & 1]
    even = [r for r in range(size) if not r & 1]
    left_odd = jnp.concatenate([left_blocks[r] for r in odd], axis=1)
    left_even = jnp.concatenate([left_blocks[r] for r in even], axis=1)
    got = swap_with(transposed_mult(left_odd, right).astype(jnp.bfloat16), "dp", size, 1)
    kept = transposed_mult(left_even, right) + got.astype(jnp.float32)
    width = kept.shape[0] // len(even)
    columns = right.shape[1]
    orders = bit_orders(size)
    cuts = {"x": [(0, columns, 0)], "y": [(0, columns, 1)], "xy": [(0, columns // 2, 0), (columns // 2, columns, 1)]}
    results = []
    for begin, end, order in cuts[routes]:
        rows_by_r = {
            r: kept[i * width : (i + 1) * width, begin:end] for i, r in enumerate(even)
        }
        results.append(halve(rows_by_r, orders[order], size))
    return results[0] if len(results) == 1 else jnp.concatenate(results, axis=1)


def local(
    sizes,
    layer_in,
    layer_cot,
    segments,
    positions,
    counts,
    attn_gain,
    w_q,
    w_k,
    value_weight,
    q_gain,
    k_gain,
    w_o,
    mlp_gain,
    w_gate,
    w_up,
    w_down,
):
    dp_size, tensor_size = sizes
    dp_index = lax.axis_index("dp")
    tensor_index = lax.axis_index("tensor")
    full_in = gather_columns(layer_in, tensor_index, tensor_size)
    full_cot = gather_columns(layer_cot, tensor_index, tensor_size)
    rows = full_in.shape[0]
    share = layer_in.shape[1]
    column_start = tensor_index * share
    q_heads = w_q.shape[1] // HEAD_SIZE
    kv_heads = w_k.shape[1] // HEAD_SIZE
    group = q_heads // kv_heads
    factor = HEAD_SIZE ** (-0.5)
    count = counts[0]
    live_rows = (jnp.arange(rows, dtype=jnp.int32) < count).astype(jnp.float32)[:, None]
    mask = allowed_mask(segments, count)
    cosine, sine = rotary_tables(positions)
    in_float = full_in.astype(jnp.float32)
    scale_one = inv_rms(in_float)
    normed_one = (in_float * scale_one * attn_gain).astype(jnp.bfloat16)
    q_lin = mult(normed_one, w_q).reshape(rows, q_heads, HEAD_SIZE)
    k_lin = mult(normed_one, w_k).reshape(rows, kv_heads, HEAD_SIZE)
    values = mult(normed_one, value_weight).astype(jnp.bfloat16).reshape(rows, kv_heads, HEAD_SIZE)

    def prep_fn(linear, gain):
        return head_prep(linear, gain, cosine, sine)

    queries_f, back_query = jax.vjp(prep_fn, q_lin, q_gain)
    keys_f, back_key = jax.vjp(prep_fn, k_lin, k_gain)
    queries = queries_f.astype(jnp.bfloat16).reshape(rows, kv_heads, group, HEAD_SIZE)
    keys = keys_f.astype(jnp.bfloat16)
    scores = scores_of(queries, keys, mask, factor)
    peak = jnp.max(scores, axis=-1, keepdims=True)
    lse = peak + jnp.log(jnp.sum(jnp.exp(scores - peak), axis=-1, keepdims=True))
    attn_probs = jnp.exp(scores - lse).astype(jnp.bfloat16)
    attended4 = jnp.einsum(
        "kgij,jkd->ikgd", attn_probs, values, preferred_element_type=jnp.float32
    ).astype(jnp.bfloat16)
    attended = attended4.reshape(rows, q_heads * HEAD_SIZE)
    attn_share = scatter_columns(mult(attended, w_o), tensor_index, tensor_size)
    attn_sum = gather_columns(attn_share.astype(jnp.bfloat16), tensor_index, tensor_size)
    residual = in_float + attn_sum.astype(jnp.float32)
    scale_two = inv_rms(residual)
    normed_two = (residual * scale_two * mlp_gain).astype(jnp.bfloat16)
    gate_lin = mult(normed_two, w_gate)
    up_lin = mult(normed_two, w_up)
    sigmoid_gate = jax.nn.sigmoid(gate_lin)
    silu_gate = gate_lin * sigmoid_gate
    hidden = (silu_gate * up_lin).astype(jnp.bfloat16)
    mlp_share = scatter_columns(mult(hidden, w_down), tensor_index, tensor_size)
    res_share = lax.dynamic_slice_in_dim(residual, column_start, share, 1)
    layer_out = ((res_share + mlp_share) * live_rows).astype(jnp.bfloat16)
    grad_out = full_cot * live_rows.astype(jnp.bfloat16)
    d_hidden = mult(grad_out, w_down.T)
    d_gate = (d_hidden * up_lin * sigmoid_gate * (1.0 + gate_lin * (1.0 - sigmoid_gate))).astype(
        jnp.bfloat16
    )
    d_up = (d_hidden * silu_gate).astype(jnp.bfloat16)
    d_two_part = mult(d_gate, w_gate.T) + mult(d_up, w_up.T)
    d_two_share = scatter_columns(d_two_part, tensor_index, tensor_size)
    d_normed_two = gather_columns(
        d_two_share.astype(jnp.bfloat16), tensor_index, tensor_size
    ).astype(jnp.float32)
    normed_two_blocks = relative_columns(normed_two, dp_index, dp_size)
    grad_out_blocks = relative_columns(grad_out, dp_index, dp_size)
    sum_w_gate = summed_gradient(normed_two_blocks, d_gate, dp_size, "x")
    sum_w_up = summed_gradient(normed_two_blocks, d_up, dp_size, "y")
    sum_w_down = summed_gradient(grad_out_blocks, hidden, dp_size, "xy").T
    local_mlp_gain = jnp.sum(d_two_part * residual * scale_two, axis=0)
    gained_two = d_normed_two * mlp_gain
    d_residual = (
        grad_out.astype(jnp.float32)
        + scale_two * gained_two
        - residual * scale_two**3 * jnp.mean(gained_two * residual, axis=-1, keepdims=True)
    )
    d_res_b = d_residual.astype(jnp.bfloat16)
    d_res_blocks = relative_columns(d_res_b, dp_index, dp_size)
    sum_w_o = summed_gradient(d_res_blocks, attended, dp_size, "xy").T
    d_attended = mult(d_res_b, w_o.T).astype(jnp.bfloat16).reshape(rows, kv_heads, group, HEAD_SIZE)
    scores_again = scores_of(queries, keys, mask, factor)
    probs_f = jnp.exp(scores_again - lse)
    delta = jnp.einsum("ikgd,ikgd->kgi", d_attended, attended4, preferred_element_type=jnp.float32)[
        ..., None
    ]
    d_probs = jnp.einsum("ikgd,jkd->kgij", d_attended, values, preferred_element_type=jnp.float32)
    d_scores = (probs_f * (d_probs - delta)).astype(jnp.bfloat16)
    d_values = jnp.einsum(
        "kgij,ikgd->jkd", attn_probs, d_attended, preferred_element_type=jnp.float32
    )
    d_queries = (
        jnp.einsum("kgij,jkd->ikgd", d_scores, keys, preferred_element_type=jnp.float32) * factor
    )
    d_keys = (
        jnp.einsum("kgij,ikgd->jkd", d_scores, queries, preferred_element_type=jnp.float32) * factor
    )
    d_q_lin, local_q_gain = back_query(d_queries.reshape(rows, q_heads, HEAD_SIZE))
    d_k_lin, local_k_gain = back_key(d_keys)
    d_q_b = d_q_lin.reshape(rows, q_heads * HEAD_SIZE).astype(jnp.bfloat16)
    d_k_b = d_k_lin.reshape(rows, kv_heads * HEAD_SIZE).astype(jnp.bfloat16)
    d_v_b = d_values.reshape(rows, kv_heads * HEAD_SIZE).astype(jnp.bfloat16)
    normed_part = mult(d_q_b, w_q.T) + mult(d_k_b, w_k.T) + mult(d_v_b, value_weight.T)
    scaled_in = in_float * scale_one
    local_attn_gain = jnp.sum(normed_part * scaled_in, axis=0)
    row_part = jnp.mean(normed_part * attn_gain * in_float, axis=-1)
    row_mean = sum(gather_pieces(row_part, tensor_size))[:, None]
    d_one_share = scatter_columns(normed_part, tensor_index, tensor_size)

    def own(array):
        return lax.dynamic_slice_in_dim(array, column_start, share, array.ndim - 1)

    in_share = layer_in.astype(jnp.float32)
    grad_in = (
        own(d_residual)
        + scale_one * own(attn_gain) * d_one_share
        - in_share * scale_one**3 * row_mean
    ).astype(jnp.bfloat16)
    normed_one_blocks = relative_columns(normed_one, dp_index, dp_size)
    sum_w_q = summed_gradient(normed_one_blocks, d_q_b, dp_size, "x")
    d_kv_b = jnp.concatenate([d_k_b, d_v_b], axis=1)
    sum_w_kv = summed_gradient(normed_one_blocks, d_kv_b, dp_size, "y")
    sum_w_k = sum_w_kv[:, : w_k.shape[1]]
    sum_w_v = sum_w_kv[:, w_k.shape[1] :]
    gains = jnp.concatenate(
        [
            vector.reshape(dp_size, -1)
            for vector in (local_attn_gain, local_mlp_gain, local_q_gain, local_k_gain)
        ],
        axis=1,
    )
    gain_rows = relative_blocks([gains[r : r + 1] for r in range(dp_size)], dp_index)
    gain_bit = dp_size // 2
    gains = jnp.concatenate(gain_rows, axis=0)
    while gain_bit >= 1:
        gains = gains[:gain_bit] + swap_with(gains[gain_bit:], "dp", dp_size, gain_bit)
        gain_bit //= 2
    gains = sum(gather_pieces(gains, tensor_size))[0]
    width = local_attn_gain.shape[0] // dp_size
    narrow = HEAD_SIZE // dp_size
    return (
        layer_out,
        grad_in,
        sum_w_q,
        sum_w_k,
        sum_w_v,
        sum_w_o,
        sum_w_gate,
        sum_w_up,
        sum_w_down,
        gains[:width],
        gains[width : 2 * width],
        gains[2 * width : 2 * width + narrow],
        gains[2 * width + narrow :],
    )


def solution(mesh):
    in_specs = (
        P("dp", "tensor"),
        P("dp", "tensor"),
        P("dp"),
        P("dp"),
        P("dp"),
        P(),
        P(None, "tensor"),
        P(None, "tensor"),
        P(None, "tensor"),
        P(),
        P(),
        P("tensor", None),
        P(),
        P(None, "tensor"),
        P(None, "tensor"),
        P("tensor", None),
    )
    out_specs = (
        P("dp", "tensor"),
        P("dp", "tensor"),
        P("dp", "tensor"),
        P("dp", "tensor"),
        P("dp", "tensor"),
        P("tensor", "dp"),
        P("dp", "tensor"),
        P("dp", "tensor"),
        P("tensor", "dp"),
        P("dp"),
        P("dp"),
        P("dp"),
        P("dp"),
    )
    sizes = (mesh.shape["dp"], mesh.shape["tensor"])

    def body(*args):
        return local(sizes, *args)

    return jax.shard_map(body, mesh=mesh, in_specs=in_specs, out_specs=out_specs, check_vma=False)
```

```python
import jax
import jax.numpy as jnp
from jax import lax
from jax.experimental import pallas as pl
from jax.experimental.pallas import tpu as pltpu
from jax.sharding import PartitionSpec as P

HEAD_SIZE = 128


EPSILON = 1e-06
THETA = 1000000.0
SMALL = 16


def swap_with(value, axis, size, bit):
    return lax.ppermute(value, axis, [(i, i ^ bit) for i in range(size)])


def relative_blocks(blocks, index):
    count = len(blocks)
    bit = 1
    while bit < count:
        flip = (index & bit) != 0
        blocks = [jnp.where(flip, blocks[r ^ bit], blocks[r]) for r in range(count)]
        bit *= 2
    return blocks


def far_first(size):
    return list(range(size - 1, 0, -1))


def gather_pieces(piece, size):
    got = {k: swap_with(piece, "tensor", size, k) for k in far_first(size)}
    return [piece] + [got[k] for k in range(1, size)]


def scatter_sum(parts):
    size = len(parts)
    got = {k: swap_with(parts[k], "tensor", size, k) for k in far_first(size)}
    total = parts[0].astype(jnp.float32)
    for k in range(1, size):
        total = total + got[k].astype(jnp.float32)
    return total


def split_columns(partial, index, size):
    share = partial.shape[1] // size
    return [
        lax.dynamic_slice_in_dim(partial, (index ^ k) * share, share, 1) for k in range(size)
    ]


def relative_columns(array, index, size):
    width = array.shape[1] // size
    return relative_blocks([array[:, r * width : (r + 1) * width] for r in range(size)], index)


def halves_of(array, index, size):
    return split_blocks(relative_columns(array, index, size))


def after(values, done):
    return lax.optimization_barrier((values, done))[0]


def bit_orders(size):
    bits = []
    bit = 2
    while bit < size:
        bits.append(bit)
        bit *= 2
    return bits, bits[::-1]


def split_blocks(blocks):
    return (
        jnp.concatenate([block for r, block in enumerate(blocks) if r & 1], axis=1),
        jnp.concatenate([block for r, block in enumerate(blocks) if not r & 1], axis=1),
    )


def mult(left, right):
    return jnp.dot(left, right, preferred_element_type=jnp.float32)


def rotary_tables(positions):
    half = HEAD_SIZE // 2
    freq = THETA ** (-(jnp.arange(half, dtype=jnp.float32) * 2.0 / HEAD_SIZE))
    angle = positions.astype(jnp.float32)[:, None] * freq[None, :]
    cosine, sine = jnp.cos(angle), jnp.sin(angle)
    return jnp.concatenate([cosine, cosine], axis=1), jnp.concatenate([-sine, sine], axis=1)


def allowed_mask(segments, count):
    rows = segments.shape[0]
    index = jnp.arange(rows, dtype=jnp.int32)
    same = segments[:, None] == segments[None, :]
    before = index[None, :] < index[:, None]
    live = index[:, None] < count
    return (index[:, None] == index[None, :]) | same & before & live


def dot_nn(left, right):
    return jnp.dot(left, right, preferred_element_type=jnp.float32)


def dot_nt(left, right):
    return lax.dot_general(
        left, right, (((1,), (1,)), ((), ())), preferred_element_type=jnp.float32
    )


def dot_tn(left, right):
    return lax.dot_general(
        left, right, (((0,), (0,)), ((), ())), preferred_element_type=jnp.float32
    )


def whole_call(kernel, scalars, arrays, outs, scratch=()):
    vmem = pl.BlockSpec(memory_space=pltpu.VMEM)
    smem = pl.BlockSpec(memory_space=pltpu.SMEM)
    return pl.pallas_call(
        kernel,
        in_specs=[smem] * len(scalars) + [vmem] * len(arrays),
        out_specs=[vmem] * len(outs),
        out_shape=[jax.ShapeDtypeStruct(shape, dtype) for shape, dtype in outs],
        scratch_shapes=list(scratch),
    )(*scalars, *arrays)


def place(index, k, share):
    return pl.ds(pl.multiple_of((index ^ k) * share, share), share)


def halves_shape(rows, width, size):
    return [((rows, width // 2), jnp.bfloat16)] * 2 if width // size % 128 == 0 else []


def write_halves(source_ref, refs, dp_index, size):
    if not refs:
        return
    block = source_ref.shape[1] // size
    for r in range(size):
        at = pl.ds(pl.multiple_of((dp_index ^ r) * block, block), block)
        refs[1 - r % 2][:, r // 2 * block : (r // 2 + 1) * block] = source_ref[:, at]


def turned(value):
    return pltpu.roll(value, HEAD_SIZE // 2, 1)


def attention_forward(dp_size, index, pieces, gain, w_q, w_k, w_v, w_o, q_gain, k_gain, cosine, sine, mask):
    size = len(pieces)
    rows, share = pieces[0].shape
    width = size * share
    q_width, k_width = w_q.shape[1], w_k.shape[1]
    q_heads, k_heads = q_width // HEAD_SIZE, k_width // HEAD_SIZE
    group = q_heads // k_heads
    factor = HEAD_SIZE ** (-0.5)

    def kernel(index_ref, *refs):
        piece_refs = refs[:size]
        (gain_r, wq_r, wk_r, wv_r, wo_r, qg_r, kg_r, cos_r, sin_r, mask_r) = refs[size : size + 10]
        out = refs[size + 10 :]
        part_refs = out[:size]
        (full_r, normed_r, scale_r, ql_r, kl_r, q_r, k_r, v_r, p_r, att_r) = out[size : size + 10]
        *half_refs, wide_r = out[size + 10 :]
        me = index_ref[0]
        for k in range(size):
            full_r[:, place(me, k, share)] = piece_refs[k][...]
        x = full_r[...].astype(jnp.float32)
        scale = lax.rsqrt(jnp.mean(x * x, axis=-1, keepdims=True) + EPSILON)
        scale_r[...] = scale
        normed_r[...] = (x * scale * gain_r[...]).astype(jnp.bfloat16)
        write_halves(normed_r, half_refs, index_ref[1], dp_size)
        normed = normed_r[...]
        ql_r[...] = dot_nn(normed, wq_r[...])
        kl_r[...] = dot_nn(normed, wk_r[...])
        v_r[...] = dot_nn(normed, wv_r[...]).astype(jnp.bfloat16)
        cos, sin = cos_r[...], sin_r[...]

        def prepared(linear, head_gain):
            inverse = lax.rsqrt(jnp.mean(linear * linear, axis=-1, keepdims=True) + EPSILON)
            u = linear * inverse * head_gain
            return (u * cos + turned(u) * sin).astype(jnp.bfloat16)

        allowed = mask_r[...] > 0.5
        for kv in range(k_heads):
            at = slice(kv * HEAD_SIZE, (kv + 1) * HEAD_SIZE)
            k_r[:, at] = prepared(kl_r[:, at], kg_r[...])
        for h in range(q_heads):
            at = slice(h * HEAD_SIZE, (h + 1) * HEAD_SIZE)
            kv_at = slice(h // group * HEAD_SIZE, (h // group + 1) * HEAD_SIZE)
            query = prepared(ql_r[:, at], qg_r[...])
            q_r[:, at] = query
            scores = jnp.where(allowed, dot_nt(query, k_r[:, kv_at]) * factor, -1e30)
            peak = jnp.max(scores, axis=-1, keepdims=True)
            lse = peak + jnp.log(jnp.sum(jnp.exp(scores - peak), axis=-1, keepdims=True))
            probs = jnp.exp(scores - lse)
            p_r[h * rows : (h + 1) * rows, :] = probs
            att_r[:, at] = dot_nn(probs.astype(jnp.bfloat16), v_r[:, kv_at]).astype(jnp.bfloat16)
        wide_r[...] = dot_nn(att_r[...], wo_r[...])
        for k in range(size):
            part_refs[k][...] = wide_r[:, place(me, k, share)].astype(jnp.bfloat16)

    bf, f32 = jnp.bfloat16, jnp.float32
    outs = [((rows, share), bf)] * size + [
        ((rows, width), bf),
        ((rows, width), bf),
        ((rows, 1), f32),
        ((rows, q_width), f32),
        ((rows, k_width), f32),
        ((rows, q_width), bf),
        ((rows, k_width), bf),
        ((rows, k_width), bf),
        ((q_heads * rows, rows), f32),
        ((rows, q_width), bf),
    ] + halves_shape(rows, width, dp_size)
    result = whole_call(
        kernel,
        [index],
        [*pieces, gain, w_q, w_k, w_v, w_o, q_gain, k_gain, cosine, sine, mask],
        outs,
        [pltpu.VMEM((rows, width), f32)],
    )
    return result[:size], result[size : size + 10], result[size + 10 :]


def feed_forward(dp_size, index, count, full_in, sum_pieces, cot_pieces, gain, w_gate, w_up, w_down):
    size = len(sum_pieces)
    rows, share = sum_pieces[0].shape
    width = size * share
    ff = w_gate.shape[1]

    def kernel(index_ref, count_ref, *refs):
        in_r = refs[0]
        sum_refs = refs[1 : 1 + size]
        cot_refs = refs[1 + size : 1 + 2 * size]
        gain_r, wg_r, wu_r, wd_r = refs[1 + 2 * size : 5 + 2 * size]
        out = refs[5 + 2 * size :]
        part_refs = out[:size]
        (res_r, normed_r, hidden_r, dgate_r, dup_r, cot_r, gain_out_r) = out[size : size + 7]
        *half_refs, wide_r = out[size + 7 :]
        me = index_ref[0]
        live = lax.broadcasted_iota(jnp.int32, (rows, 1), 0) < count_ref[0]
        zero = jnp.zeros((rows, share), jnp.bfloat16)
        for k in range(size):
            at = place(me, k, share)
            wide_r[:, at] = sum_refs[k][...].astype(jnp.float32)
            cot_r[:, at] = jnp.where(live, cot_refs[k][...], zero)
        residual = in_r[...].astype(jnp.float32) + wide_r[...]
        res_r[...] = residual
        scale = lax.rsqrt(jnp.mean(residual * residual, axis=-1, keepdims=True) + EPSILON)
        normed_r[...] = (residual * scale * gain_r[...]).astype(jnp.bfloat16)
        normed = normed_r[...]
        gate = dot_nn(normed, wg_r[...])
        up = dot_nn(normed, wu_r[...])
        sigmoid = jax.nn.sigmoid(gate)
        silu = gate * sigmoid
        hidden_r[...] = (silu * up).astype(jnp.bfloat16)
        d_hidden = dot_nt(cot_r[...], wd_r[...])
        dgate_r[...] = (d_hidden * up * sigmoid * (1.0 + gate * (1.0 - sigmoid))).astype(
            jnp.bfloat16
        )
        dup_r[...] = (d_hidden * silu).astype(jnp.bfloat16)
        part = dot_nt(dgate_r[...], wg_r[...]) + dot_nt(dup_r[...], wu_r[...])
        wide_r[...] = part
        for k in range(size):
            part_refs[k][...] = wide_r[:, place(me, k, share)].astype(jnp.bfloat16)
        write_halves(normed_r, half_refs[:2], index_ref[1], dp_size)
        write_halves(cot_r, half_refs[2:], index_ref[1], dp_size)
        gain_out_r[...] = jnp.sum(part * res_r[...] * scale, axis=0, keepdims=True)

    bf, f32 = jnp.bfloat16, jnp.float32
    outs = [((rows, share), bf)] * size + [
        ((rows, width), f32),
        ((rows, width), bf),
        ((rows, ff), bf),
        ((rows, ff), bf),
        ((rows, ff), bf),
        ((rows, width), bf),
        ((1, width), f32),
    ] + halves_shape(rows, width, dp_size) * 2
    result = whole_call(
        kernel,
        [index, count],
        [full_in, *sum_pieces, *cot_pieces, gain, w_gate, w_up, w_down],
        outs,
        [pltpu.VMEM((rows, width), f32)],
    )
    return result[:size], result[size : size + 7], result[size + 7 :]


def attention_backward(
    dp_size, index, d_pieces, residual, grad_out, mlp_gain, local_mlp_gain, saved, attn_gain, w_q, w_k, w_v, w_o, q_gain,
    k_gain, cosine, sine,
):
    full_in, scale_one, q_lin, k_lin, queries, keys, values, probs, attended = saved
    size = len(d_pieces)
    rows, share = d_pieces[0].shape
    width = size * share
    q_width, k_width = w_q.shape[1], w_k.shape[1]
    q_heads, k_heads = q_width // HEAD_SIZE, k_width // HEAD_SIZE
    group = q_heads // k_heads
    factor = HEAD_SIZE ** (-0.5)

    def kernel(index_ref, *refs):
        d_refs = refs[:size]
        (
            res_r, cot_r, mg_r, lg_r, in_r, sc_r, ql_r, kl_r, q_r, k_r, v_r, p_r, att_r, ag_r, wq_r,
            wk_r, wv_r, wo_r, qg_r, kg_r, cos_r, sin_r,
        ) = refs[size : size + 22]
        out = refs[size + 22 :]
        part_refs = out[:size]
        (own_r, dres_r, dq_r, dkv_r, small_r) = out[size : size + 5]
        *half_refs, wide_r, datt_r = out[size + 5 :]
        me = index_ref[0]
        for k in range(size):
            wide_r[:, place(me, k, share)] = d_refs[k][...].astype(jnp.float32)
        residual = res_r[...]
        scale = lax.rsqrt(jnp.mean(residual * residual, axis=-1, keepdims=True) + EPSILON)
        gained = wide_r[...] * mg_r[...]
        d_residual = (
            cot_r[...].astype(jnp.float32)
            + scale * gained
            - residual * (scale * scale * scale) * jnp.mean(gained * residual, axis=-1, keepdims=True)
        )
        wide_r[...] = d_residual
        own_r[...] = wide_r[:, place(me, 0, share)]
        dres_r[...] = d_residual.astype(jnp.bfloat16)
        write_halves(dres_r, half_refs, index_ref[1], dp_size)
        datt_r[...] = dot_nt(dres_r[...], wo_r[...]).astype(jnp.bfloat16)
        cos, sin = cos_r[...], sin_r[...]

        def prepared_back(linear, head_gain, d_out):
            inverse = lax.rsqrt(jnp.mean(linear * linear, axis=-1, keepdims=True) + EPSILON)
            d_u = d_out * cos + turned(d_out * sin)
            d_gain = jnp.sum(d_u * linear * inverse, axis=0, keepdims=True)
            d_n = d_u * head_gain
            mean = jnp.mean(d_n * linear, axis=-1, keepdims=True)
            return inverse * d_n - linear * (inverse * inverse * inverse * mean), d_gain

        q_gain_sum = jnp.zeros((1, HEAD_SIZE), jnp.float32)
        k_gain_sum = jnp.zeros((1, HEAD_SIZE), jnp.float32)
        for kv in range(k_heads):
            kv_at = slice(kv * HEAD_SIZE, (kv + 1) * HEAD_SIZE)
            key, value = k_r[:, kv_at], v_r[:, kv_at]
            d_key = jnp.zeros((rows, HEAD_SIZE), jnp.float32)
            d_value = jnp.zeros((rows, HEAD_SIZE), jnp.float32)
            for g in range(group):
                h = kv * group + g
                at = slice(h * HEAD_SIZE, (h + 1) * HEAD_SIZE)
                d_att = datt_r[:, at]
                delta = jnp.sum(
                    d_att.astype(jnp.float32) * att_r[:, at].astype(jnp.float32),
                    axis=-1,
                    keepdims=True,
                )
                prob = p_r[h * rows : (h + 1) * rows, :]
                d_score = (prob * (dot_nt(d_att, value) - delta)).astype(jnp.bfloat16)
                d_value = d_value + dot_tn(prob.astype(jnp.bfloat16), d_att)
                d_key = d_key + dot_tn(d_score, q_r[:, at])
                d_linear, d_gain = prepared_back(
                    ql_r[:, at], qg_r[...], dot_nn(d_score, key) * factor
                )
                q_gain_sum = q_gain_sum + d_gain
                dq_r[:, at] = d_linear.astype(jnp.bfloat16)
            d_linear, d_gain = prepared_back(kl_r[:, kv_at], kg_r[...], d_key * factor)
            k_gain_sum = k_gain_sum + d_gain
            dkv_r[:, kv_at] = d_linear.astype(jnp.bfloat16)
            dkv_r[:, k_width + kv * HEAD_SIZE : k_width + (kv + 1) * HEAD_SIZE] = d_value.astype(
                jnp.bfloat16
            )
        part = (
            dot_nt(dq_r[...], wq_r[...])
            + dot_nt(dkv_r[:, :k_width], wk_r[...])
            + dot_nt(dkv_r[:, k_width:], wv_r[...])
        )
        wide_r[...] = part
        weighted = part * in_r[...].astype(jnp.float32)
        gain_sum = jnp.sum(weighted * sc_r[...], axis=0, keepdims=True)
        row = jnp.mean(weighted * ag_r[...], axis=-1, keepdims=True)
        row = jnp.broadcast_to(row, (rows, HEAD_SIZE)).T[:1, :]
        small_r[...] = jnp.zeros(small_r.shape, jnp.float32)
        at = 0
        for vector in (row, gain_sum, lg_r[...]):
            for begin in range(0, vector.shape[1], share):
                small_r[at : at + 1, :] = vector[:, begin : begin + share]
                at += 1
        small_r[at : at + 1, :HEAD_SIZE] = q_gain_sum
        small_r[at : at + 1, HEAD_SIZE : 2 * HEAD_SIZE] = k_gain_sum
        small = small_r[...]
        high = small.astype(jnp.bfloat16)
        low = (small - high.astype(jnp.float32)).astype(jnp.bfloat16)
        for k in range(size):
            part_refs[k][:rows, :] = wide_r[:, place(me, k, share)].astype(jnp.bfloat16)
            part_refs[k][rows : rows + SMALL, :] = high
            part_refs[k][rows + SMALL :, :] = low

    bf, f32 = jnp.bfloat16, jnp.float32
    outs = [((rows + 2 * SMALL, share), bf)] * size + [
        ((rows, share), f32),
        ((rows, width), bf),
        ((rows, q_width), bf),
        ((rows, 2 * k_width), bf),
        ((SMALL, share), f32),
    ] + halves_shape(rows, width, dp_size)
    result = whole_call(
        kernel,
        [index],
        [
            *d_pieces, residual, grad_out, mlp_gain, local_mlp_gain, full_in, scale_one, q_lin, k_lin, queries,
            keys, values, probs, attended, attn_gain, w_q, w_k, w_v, w_o, q_gain, k_gain, cosine,
            sine,
        ],
        outs,
        [pltpu.VMEM((rows, width), f32), pltpu.VMEM((rows, q_width), bf)],
    )
    return result[:size], result[size : size + 5], result[size + 5 :]


def input_gradient(index, own, gots, small, d_res_own, layer_in, scale_one, attn_gain):
    rows, share = layer_in.shape

    def kernel(index_ref, *refs):
        own_r, got_refs = refs[0], refs[1 : 1 + len(gots)]
        small_r, dres_r, in_r, sc_r, ag_r, out_r, total_r = refs[1 + len(gots) :]
        d_normed = own_r[:rows, :].astype(jnp.float32)
        total = small_r[...]
        for got_r in got_refs:
            d_normed = d_normed + got_r[:rows, :].astype(jnp.float32)
            total = total + (
                got_r[rows : rows + SMALL, :].astype(jnp.float32)
                + got_r[rows + SMALL :, :].astype(jnp.float32)
            )
        total_r[...] = total
        mean = jnp.broadcast_to(total[:1, :], (HEAD_SIZE, share)).T[:, :1]
        scale = sc_r[...]
        gain = ag_r[:, place(index_ref[0], 0, share)]
        out_r[...] = (
            dres_r[...]
            + scale * (gain * d_normed)
            - in_r[...].astype(jnp.float32) * (scale * scale * scale) * mean
        ).astype(jnp.bfloat16)

    return whole_call(
        kernel,
        [index],
        [own, *gots, small, d_res_own, layer_in, scale_one, attn_gain],
        [((rows, share), jnp.bfloat16), ((SMALL, share), jnp.float32)],
    )


def first_messages(lefts, rights):
    count = len(lefts)

    def kernel(*refs):
        for left, right, out in zip(refs[:count], refs[count : 2 * count], refs[2 * count :]):
            out[...] = dot_tn(left[...], right[...]).astype(jnp.bfloat16)

    outs = [
        ((left.shape[1], right.shape[1]), jnp.bfloat16) for left, right in zip(lefts, rights)
    ]
    return whole_call(kernel, [], [*lefts, *rights], outs)


def second_messages(lefts, rights, gots, routes, keys, bits):
    count = len(lefts)
    rows = lefts[0].shape[1] // len(keys)

    def kernel(*refs):
        left_r, right_r, got_r = refs[:count], refs[count : 2 * count], refs[2 * count : 3 * count]
        out = refs[3 * count :]
        for p in range(count):
            total = dot_tn(left_r[p][...], right_r[p][...]) + got_r[p][...].astype(jnp.float32)
            for d, route in enumerate(routes):
                message_r, rest_r = out[2 * d], out[2 * d + 1]
                offset = 0
                for product, begin, end in route:
                    if product == p:
                        sent = kept = 0
                        for i, r in enumerate(keys):
                            block = total[i * rows : (i + 1) * rows, begin:end]
                            columns = slice(offset, offset + end - begin)
                            if r & bits[d]:
                                message_r[sent * rows : (sent + 1) * rows, columns] = block.astype(
                                    jnp.bfloat16
                                )
                                sent += 1
                            else:
                                rest_r[kept * rows : (kept + 1) * rows, columns] = block
                                kept += 1
                    offset += end - begin

    outs = []
    for route in routes:
        shape = (rows * len(keys) // 2, sum(end - begin for _, begin, end in route))
        outs += [(shape, jnp.bfloat16), (shape, jnp.float32)]
    return whole_call(kernel, [], [*lefts, *rights, *gots], outs)


def third_messages(rests, gots, keys, bits):
    count = len(rests)
    widths = [rest.shape[0] // len(key) for rest, key in zip(rests, keys)]

    def kernel(*refs):
        for d in range(count):
            total = refs[d][...] + refs[count + d][...].astype(jnp.float32)
            message_r, rest_r = refs[2 * count + 2 * d], refs[2 * count + 2 * d + 1]
            rows = widths[d]
            sent = kept = 0
            for i, r in enumerate(keys[d]):
                block = total[i * rows : (i + 1) * rows, :]
                if r & bits[d]:
                    message_r[sent * rows : (sent + 1) * rows, :] = block.astype(jnp.bfloat16)
                    sent += 1
                else:
                    rest_r[kept * rows : (kept + 1) * rows, :] = block
                    kept += 1

    outs = []
    for rest in rests:
        shape = (rest.shape[0] // 2, rest.shape[1])
        outs += [(shape, jnp.bfloat16), (shape, jnp.float32)]
    return whole_call(kernel, [], [*rests, *gots], outs)


def last_sums(rests, gots, outputs):
    count = len(rests)
    rows = rests[0].shape[0]
    outs = []
    for transposed, pieces in outputs:
        columns = sum(end - begin for _, begin, end in pieces)
        outs.append(((columns, rows) if transposed else (rows, columns), jnp.float32))

    def kernel(*refs):
        totals = [refs[d][...] + refs[count + d][...].astype(jnp.float32) for d in range(count)]
        for out_r, (transposed, pieces) in zip(refs[2 * count :], outputs):
            offset = 0
            for d, begin, end in pieces:
                block = totals[d][:, begin:end]
                if transposed:
                    out_r[offset : offset + end - begin, :] = block.T
                else:
                    out_r[:, offset : offset + end - begin] = block
                offset += end - begin

    if rows % 128 == 0:
        return whole_call(kernel, [], [*rests, *gots], outs)
    totals = [rest + got.astype(jnp.float32) for rest, got in zip(rests, gots)]
    results = []
    for transposed, pieces in outputs:
        joined = jnp.concatenate([totals[d][:, begin:end] for d, begin, end in pieces], axis=1)
        results.append(joined.T if transposed else joined)
    return results


def reduced(lefts, rights, gots, routes, outputs, size):
    keys = [r for r in range(size) if not r & 1]
    orders = bit_orders(size)
    bits = [order[0] for order in orders]
    message_x, rest_x, message_y, rest_y = second_messages(lefts, rights, gots, routes, keys, bits)
    rests = [rest_x, rest_y]
    gots = [
        swap_with(message, "dp", size, bit)
        for message, bit in zip((message_x, message_y), bits)
    ]
    keys = [[r for r in keys if not r & bit] for bit in bits]
    for stage in range(1, len(orders[0])):
        bits = [order[stage] for order in orders]
        message_x, rest_x, message_y, rest_y = third_messages(rests, gots, keys, bits)
        rests = [rest_x, rest_y]
        gots = [
            swap_with(message, "dp", size, bit)
            for message, bit in zip((message_x, message_y), bits)
        ]
        keys = [[r for r in key if not r & bit] for key, bit in zip(keys, bits)]
    return last_sums(rests, gots, outputs)


def local(
    sizes,
    layer_in,
    layer_cot,
    segments,
    positions,
    counts,
    attn_gain,
    w_q,
    w_k,
    value_weight,
    q_gain,
    k_gain,
    w_o,
    mlp_gain,
    w_gate,
    w_up,
    w_down,
):
    dp_size, tensor_size = sizes
    dp_index = lax.axis_index("dp")
    tensor_index = lax.axis_index("tensor")
    index = jnp.stack([tensor_index, dp_index]).astype(jnp.int32)
    rows, share = layer_in.shape
    width = w_q.shape[0]
    ff = w_gate.shape[1]
    in_pieces = gather_pieces(layer_in, tensor_size)
    live_rows = (jnp.arange(rows, dtype=jnp.int32) < counts[0]).astype(jnp.float32)[:, None]
    mask = allowed_mask(segments, counts[0]).astype(jnp.float32)
    cosine, sine = rotary_tables(positions)
    attn_gain_row = attn_gain.reshape(1, width)
    mlp_gain_row = mlp_gain.reshape(1, width)
    q_gain_row = q_gain.reshape(1, HEAD_SIZE)
    k_gain_row = k_gain.reshape(1, HEAD_SIZE)
    cot_pieces = gather_pieces(after(layer_cot, (mask, cosine, sine)), tensor_size)
    parts, kept, one_halves = attention_forward(
        dp_size, index, in_pieces, attn_gain_row, w_q, w_k, value_weight, w_o, q_gain_row, k_gain_row,
        cosine, sine, mask,
    )
    full_in, normed_one, scale_one, q_lin, k_lin, queries, keys, values, probs, attended = kept
    attn_share = scatter_sum(parts).astype(jnp.bfloat16)
    sum_pieces = gather_pieces(attn_share, tensor_size)
    parts, kept, two_halves = feed_forward(
        dp_size, index, counts, full_in, sum_pieces, cot_pieces, mlp_gain_row, w_gate, w_up, w_down
    )
    residual, normed_two, hidden, d_gate, d_up, grad_out, local_mlp_gain = kept
    d_two_share = scatter_sum(parts).astype(jnp.bfloat16)
    normed_two_odd, normed_two_even = two_halves[:2] or halves_of(normed_two, dp_index, dp_size)
    grad_out_odd, grad_out_even = two_halves[2:] or halves_of(grad_out, dp_index, dp_size)
    rights = [d_gate, d_up, hidden]
    sent = first_messages([normed_two_odd, normed_two_odd, grad_out_odd], rights)
    got = [swap_with(array, "dp", dp_size, 1) for array in sent]
    mlp_parts = split_columns(mult(hidden, w_down).astype(jnp.bfloat16), tensor_index, tensor_size)
    d_two_pieces = gather_pieces(d_two_share, tensor_size)
    half = ff // 2
    sum_w_gate, sum_w_up, sum_w_down = reduced(
        [normed_two_even, normed_two_even, grad_out_even],
        rights,
        got,
        [[(0, 0, ff), (2, 0, half)], [(1, 0, ff), (2, half, ff)]],
        [
            (False, [(0, 0, ff)]),
            (False, [(1, 0, ff)]),
            (True, [(0, ff, ff + half), (1, ff, ff + half)]),
        ],
        dp_size,
    )
    mlp_parts = after(mlp_parts, d_two_pieces[:2])
    mlp_share = scatter_sum(mlp_parts)
    res_share = layer_in.astype(jnp.float32) + attn_share.astype(jnp.float32)
    layer_out = ((res_share + mlp_share) * live_rows).astype(jnp.bfloat16)
    parts, kept, res_halves = attention_backward(
        dp_size,
        index,
        d_two_pieces,
        residual,
        grad_out,
        mlp_gain_row,
        local_mlp_gain,
        (full_in, scale_one, q_lin, k_lin, queries, keys, values, probs, attended),
        attn_gain_row,
        w_q,
        w_k,
        value_weight,
        w_o,
        q_gain_row,
        k_gain_row,
        cosine,
        sine,
    )
    d_res_own, d_res_b, d_q_b, d_kv_b, small = kept
    one_pieces = {k: swap_with(parts[k], "tensor", tensor_size, k) for k in far_first(tensor_size)}
    grad_in, small = input_gradient(
        index,
        parts[0],
        [one_pieces[k] for k in range(1, tensor_size)],
        small,
        d_res_own,
        layer_in,
        scale_one,
        attn_gain_row,
    )
    normed_one_odd, normed_one_even = one_halves or halves_of(normed_one, dp_index, dp_size)
    d_res_odd, d_res_even = res_halves or halves_of(d_res_b, dp_index, dp_size)
    rights = [d_q_b, d_kv_b, attended]
    sent = first_messages([normed_one_odd, normed_one_odd, d_res_odd], rights)
    got = [swap_with(array, "dp", dp_size, 1) for array in sent]
    q_end, kv_end, o_end = (right.shape[1] for right in rights)
    k_end = w_k.shape[1]
    half = o_end // 2
    sum_w_q, sum_w_k, sum_w_v, sum_w_o = reduced(
        [normed_one_even, normed_one_even, d_res_even],
        rights,
        got,
        [[(0, 0, q_end), (2, 0, half)], [(1, 0, kv_end), (2, half, o_end)]],
        [
            (False, [(0, 0, q_end)]),
            (False, [(1, 0, k_end)]),
            (False, [(1, k_end, kv_end)]),
            (True, [(0, q_end, q_end + half), (1, kv_end, kv_end + half)]),
        ],
        dp_size,
    )

    used = 2 * (width // share)
    gains = small[1 : 1 + used].reshape(2, dp_size, -1)
    head_gains = small[1 + used : 2 + used, : 2 * HEAD_SIZE]
    gains = jnp.concatenate([gains[0], gains[1]], axis=1)
    gains = jnp.concatenate(
        relative_blocks([gains[r : r + 1] for r in range(dp_size)], dp_index), axis=0
    )
    wide = width // dp_size
    narrow = HEAD_SIZE // dp_size
    head_gains = jnp.pad(head_gains, ((0, 0), (0, max(0, 2 * wide - 2 * HEAD_SIZE))))
    gains = jnp.pad(gains, ((0, 0), (0, max(0, 2 * HEAD_SIZE - 2 * wide))))
    bit = dp_size // 2
    while bit >= 1:
        message = jnp.concatenate([gains[bit:], head_gains], axis=0)
        message = swap_with(message, "dp", dp_size, bit)
        gains = gains[:bit] + message[:bit]
        head_gains = head_gains + message[bit:]
        bit //= 2
    q_gain_sum = lax.dynamic_slice_in_dim(head_gains[0], dp_index * narrow, narrow, 0)
    k_gain_sum = lax.dynamic_slice_in_dim(head_gains[0], HEAD_SIZE + dp_index * narrow, narrow, 0)
    return (
        layer_out,
        grad_in,
        sum_w_q,
        sum_w_k,
        sum_w_v,
        sum_w_o,
        sum_w_gate,
        sum_w_up,
        sum_w_down,
        gains[0, :wide],
        gains[0, wide : 2 * wide],
        q_gain_sum,
        k_gain_sum,
    )


def solution(mesh):
    in_specs = (
        P("dp", "tensor"),
        P("dp", "tensor"),
        P("dp"),
        P("dp"),
        P("dp"),
        P(),
        P(None, "tensor"),
        P(None, "tensor"),
        P(None, "tensor"),
        P(),
        P(),
        P("tensor", None),
        P(),
        P(None, "tensor"),
        P(None, "tensor"),
        P("tensor", None),
    )
    out_specs = (
        P("dp", "tensor"),
        P("dp", "tensor"),
        P("dp", "tensor"),
        P("dp", "tensor"),
        P("dp", "tensor"),
        P("tensor", "dp"),
        P("dp", "tensor"),
        P("dp", "tensor"),
        P("tensor", "dp"),
        P("dp"),
        P("dp"),
        P("dp"),
        P("dp"),
    )
    sizes = (mesh.shape["dp"], mesh.shape["tensor"])

    def body(*args):
        return local(sizes, *args)

    return jax.shard_map(body, mesh=mesh, in_specs=in_specs, out_specs=out_specs, check_vma=False)
```
